32 devices in a mesh: dp: 4 (over x, core), expert: 8 (over z, y).
Axes of the slice: x: 2, y: 2, z: 4, core: 2. Of those that a mesh axis runs over, the one named last changes fastest.
Arguments:
- hidden: bfloat16 [2048, 8, 1536], P(('dp', 'expert')), may hold values from -6 to 6
- routes: int32 [2048, 8], P(('dp', 'expert')), may hold values from 0 to 15, all different within a row; in each aligned block of 64 rows (0 to 63, 64 to 127, ...) at most 48 rows name the same one
- gate_scores: int32 [2048, 8], P(('dp', 'expert')), may hold values from 1 to 64
- down_weight: bfloat16 [16, 1536, 4096], P('expert', None, 'dp'), may hold values from -0.15625 to 0.15625
Outputs:
- output: bfloat16 [2048, 4096], P(('dp', 'expert'))
- gram: float32 [16, 1536, 1536], P('expert', 'dp')
The draws below stay inside these ranges and needn't reach their ends.
Inputs may be any that keep to these rules, and one draw needn't show every extreme that they name: `routes`: each token names 8 different experts. Among the 64 tokens of one device no expert is named more than 48 times, and on some devices one expert is named exactly 48 times. Every expert is named by some token.
All inputs are finite; a program needn't handle non-finite values.
Results may differ from the reference program's by a relative error of at most 0.005.
Values may be sent and summed in bfloat16 or wider, within the bound.
A program may use at most 128 MiB of HBM per device.

```python
import math
import jax
import jax.numpy as jnp
import numpy as np
from jax import lax

D = 4096
FF = 1536
TOPK = 8
TOK_DEV = 64
EXPERTS = 16
CAP = 48
TOKENS = 2048
N_DP = 4
N_EXPERT = 8


def touch_ends(entries, stream_key, low, largest):
    index_at = [jax.random.randint(jax.random.fold_in(stream_key, axis), (), 0, length) for axis, length in enumerate(entries.shape)]
    longest = entries.shape.index(max(entries.shape))
    next_to = index_at[:longest] + [(index_at[longest] + 1) % entries.shape[longest]] + index_at[longest + 1:]
    return entries.at[tuple(index_at)].set(low).at[tuple(next_to)].set(largest)


def level_of(rng, dims, cuts, low, largest):
    def one(dim, blocks):
        steps = jax.random.uniform(jax.random.fold_in(jax.random.fold_in(rng, 6), dim), (blocks,), jnp.float32, low / len(cuts), largest / len(cuts))
        return jnp.repeat(jnp.exp(steps), dims[dim] // blocks).reshape((-1,) + (1,) * (len(dims) - dim - 1))

    loudness = one(*cuts[0])
    for cut in cuts[1:]:
        loudness = loudness * one(*cut)
    return loudness


def shared_out(rng, own, number, rows, amount, top, reach, slope):
    ranking = jax.random.permutation(rng, amount)
    crowded, common = shares(amount, rows * top, reach, slope, True), shares(amount, rows * top, reach, slope, False)
    places = jnp.arange(amount)

    def named(tallies, rotation):
        used = int((tallies > 0).sum())
        fixed = max(1, used // 4)
        passed = fixed + (places - fixed + rotation * (used - fixed)) % max(1, amount - fixed)
        return jnp.zeros((amount,), jnp.int32).at[ranking[jnp.where(places < fixed, places, passed)]].set(jnp.asarray(tallies, jnp.int32))

    tallies = jnp.where(number % 4 == 0, named(crowded, number // 4), named(common, number - number // 4 - 1))
    mixed = jax.random.permutation(jax.random.fold_in(own, 3), amount)
    giver, receiver = mixed[0:amount // 2 * 2:2], mixed[1:amount // 2 * 2:2]
    room = jnp.minimum(tallies[giver] - 1, reach - tallies[receiver]) // 2
    room = jnp.where((giver == ranking[0]) | (receiver == ranking[0]) | (tallies[receiver] == 0), 0, jnp.maximum(room, 0))
    passed = jax.random.randint(jax.random.fold_in(own, 4), (amount // 2,), 0, 1 << 20) % (room + 1)
    tallies = tallies.at[giver].add(-passed).at[receiver].add(passed)
    members = jnp.searchsorted(jnp.cumsum(tallies), jnp.arange(rows * top), side="right").astype(jnp.int32)
    grid = members.reshape(top, rows).T
    grid = grid[jax.random.permutation(jax.random.fold_in(own, 1), rows)]
    rotation = jax.random.randint(jax.random.fold_in(own, 2), (rows, 1), 0, top)
    return jnp.take_along_axis(grid, (jnp.arange(top)[None, :] + rotation) % top, axis=1)


def shares(count, total, reach, slope, full):
    weights = [(1 << 20) // math.isqrt(standing ** slope) + 1 for standing in range(1, count + 1)]
    largest = reach if full else min(reach, max(-(-total // count), total * weights[0] // sum(weights)))
    least = 1 if total - largest >= count - 1 else 0
    given, rest = [largest] + [least] * (count - 1), total - largest - least * (count - 1)
    while rest > 0:
        movable = [i for i in range(1, count) if given[i] < largest] or [i for i in range(1, count) if given[i] < reach]
        pool, remaining = sum([weights[i] for i in movable]), rest
        for i in movable:
            addition = min(reach - given[i], max(1, remaining * weights[i] // pool), rest)
            given[i] = given[i] + addition
            rest = rest - addition
    return np.array(given)


def gaussian(stream_key, shape, deviation, limit, pieces=(), held_as=jnp.bfloat16):
    values = jax.random.normal(stream_key, shape, jnp.float32) * deviation
    if len(pieces) > 0:
        values = level_of(stream_key, shape, pieces, -0.22, 0.18) * values
    return jnp.clip(values, min=-limit, max=limit).astype(held_as)


def setup_inputs(seed: int = 0) -> dict:
    streams_of = jax.random.split(jax.random.key(seed), 5)
    hidden = gaussian(streams_of[0], (TOKENS, TOPK, FF), 1.0, 6.0, ((0, 32),))
    routes_keys = jax.random.split(jax.random.fold_in(streams_of[1], 1), TOKENS // TOK_DEV)
    routes_turns = jax.random.permutation(jax.random.fold_in(streams_of[1], 3), TOKENS // TOK_DEV)
    routes = jax.vmap(lambda own, number: shared_out(jax.random.fold_in(streams_of[1], 2), own, number, TOK_DEV, EXPERTS, TOPK, CAP, 2))(routes_keys, routes_turns).reshape((TOKENS, TOPK))
    gate_scores = touch_ends(jax.random.randint(streams_of[2], (TOKENS, TOPK), 1, 65), jax.random.fold_in(streams_of[2], 1), 1, 64).astype(jnp.int32)
    down_weight = gaussian(streams_of[3], (EXPERTS, FF, D), FF ** -0.5, 0.15625, ((0, 8), (2, 4)))
    return {"hidden": hidden, "routes": routes, "gate_scores": gate_scores, "down_weight": down_weight}


def reference(hidden, routes, gate_scores, down_weight):
    experts = down_weight.shape[0]
    model_width = down_weight.shape[2]
    tokens = hidden.shape[0]
    top_count = hidden.shape[1]
    hidden_width = hidden.shape[2]
    pair_total = tokens * top_count
    flat_routes = routes.reshape(pair_total).astype(jnp.int32)
    pair_rows = hidden.reshape(pair_total, hidden_width)
    sort_order = jnp.argsort(flat_routes, stable=True).astype(jnp.int32)
    counts = jnp.zeros((experts,), jnp.int32).at[flat_routes].add(1)
    starts = (jnp.cumsum(counts) - counts).astype(jnp.int32)
    span_rows = N_DP * N_EXPERT * CAP
    padded_rows = jnp.concatenate([pair_rows[sort_order], jnp.zeros((span_rows, hidden_width), pair_rows.dtype)], axis=0)
    owner_token = jnp.concatenate([(sort_order // top_count).astype(jnp.int32), jnp.full((span_rows,), tokens, jnp.int32)])
    scores = gate_scores.astype(jnp.float32)
    weight = scores / jnp.sum(scores, axis=1, keepdims=True)
    padded_weight = jnp.concatenate([weight.reshape(pair_total)[sort_order], jnp.zeros((span_rows,), jnp.float32)])

    def per_expert(accumulated, expert):
        first_row = starts[expert]
        segment = lax.dynamic_slice_in_dim(padded_rows, first_row, span_rows, 0)
        live_rows = jnp.arange(span_rows, dtype=jnp.int32) < counts[expert]
        segment = jnp.where(live_rows[:, None], segment, jnp.zeros_like(segment))
        gram_block = jnp.dot(segment.T, segment, preferred_element_type=jnp.float32) / counts[expert].astype(jnp.float32)
        contrib = jnp.dot(segment, down_weight[expert], preferred_element_type=jnp.float32).astype(jnp.bfloat16)
        pair_weights = lax.dynamic_slice_in_dim(padded_weight, first_row, span_rows, 0)
        target = lax.dynamic_slice_in_dim(owner_token, first_row, span_rows, 0)
        target = jnp.where(live_rows, target, tokens)
        accumulated = accumulated.at[target].add(contrib.astype(jnp.float32) * pair_weights[:, None], mode="drop")
        return accumulated, gram_block

    accumulated, grams = lax.scan(per_expert, jnp.zeros((tokens, model_width), jnp.float32), jnp.arange(experts, dtype=jnp.int32))
    return accumulated.astype(jnp.bfloat16), grams
```

```python
import functools

import jax
import jax.numpy as jnp
from jax import lax
from jax.experimental import pallas as pl
from jax.experimental.pallas import tpu as pltpu
from jax.sharding import PartitionSpec as P

MESH = pl.DeviceIdType.MESH
META = 128
TILE = 256
VMEM_BUDGET = 58 * 2**20
VMEM_LIMIT = 63 * 2**20


def fused_kernel(
    nd, ne, tokens, cap, width,
    og, w_hbm, o_ref, g_ref, c_ref,
    buf, w, sendy, recvy, keep, sendz, recvz, fin, osc, chi, clo,
    wsem, lsem, asend, xsend, csend, recv, ysend, yrecv, zsend, zrecv, osend, orecv,
):
    po = w.shape[0]
    nz = ne // 2
    nx = nd // 2
    rows = nd * cap
    group = nd * tokens
    cols = w.shape[2]
    d = lax.axis_index("dp")
    e = lax.axis_index("expert")
    x, c = lax.div(d, 2), lax.rem(d, 2)
    z, y = lax.div(e, 2), lax.rem(e, 2)
    other = d + 1 - 2 * c
    pair = e + 1 - 2 * y

    load_w = pltpu.make_async_copy(w_hbm, w, wsem)
    load_w.start()

    def slot_of(dd, ee):
        return buf.at[:, pl.ds(pl.multiple_of((ee * nd + dd) * cap, cap), cap), :]

    own = pltpu.make_async_copy(
        og.at[pl.ds(e * po, po)], slot_of(d, e), lsem
    )
    own.start()

    barrier = pltpu.get_barrier_semaphore()
    for k in range(1, ne):
        pl.semaphore_signal(
            barrier, inc=1, device_id=(d, lax.rem(e + k, ne)), device_id_type=MESH
        )
    for k in range(1, nd):
        pl.semaphore_signal(
            barrier, inc=1, device_id=(lax.rem(d + k, nd), e), device_id_type=MESH
        )
    pl.semaphore_wait(barrier, ne - 1 + nd - 1)

    def remote(src, dst, ss, rs, dd, ee):
        return pltpu.make_async_remote_copy(
            src_ref=src, dst_ref=dst, send_sem=ss, recv_sem=rs,
            device_id=(dd, ee), device_id_type=MESH,
        )

    def first(i):
        kz, ky = (i // 2 + 1) % nz, i % 2
        target = lax.rem(z + kz, nz) * 2 + lax.rem(y + ky, 2)
        return remote(
            og.at[pl.ds(target * po, po)], slot_of(d, e), asend.at[i],
            recv.at[e * nd + d], d, target,
        )

    for i in range(ne):
        if i != ne - 2:
            first(i).start()
    own.wait()
    c_ref[...] = jnp.zeros_like(c_ref)

    def source_of(i):
        kz = lax.rem(lax.div(i, 2) + 1, nz)
        zi = lax.rem(z - kz + nz, nz)
        return zi, zi * 2 + lax.rem(y + lax.rem(i, 2), 2)

    def arrived(dd, ee):
        here = slot_of(dd, ee)
        remote(here, here, asend.at[0], recv.at[ee * nd + dd], d, e).wait_recv()

    def to_x(i, j, ee):
        here = slot_of(d, ee)
        return remote(
            here, here, xsend.at[i, j], recv.at[ee * nd + d],
            lax.rem(x + j + 1, nx) * 2 + c, e,
        )

    def to_core(i, j, ee):
        dd = lax.rem(x + j, nx) * 2 + c
        here = slot_of(dd, ee)
        return remote(here, here, csend.at[i, j], recv.at[ee * nd + dd], other, e)

    def to_pair(zi):
        return remote(sendy.at[zi], recvy.at[zi], ysend.at[zi], yrecv.at[zi], d, pair)

    def to_line(zi):
        return remote(
            sendz.at[zi], recvz.at[z], zsend.at[zi], zrecv.at[z], d, zi * 2 + y
        )

    def from_pair(zi):
        remote(sendy.at[zi], recvy.at[zi], ysend.at[zi], yrecv.at[zi], d, e).wait_recv()

    def work(i):
        zi, ee = source_of(i)
        mine = lax.rem(i, 2) == 0
        span = pl.ds(pl.multiple_of(ee * rows, rows), rows)
        row = lax.broadcasted_iota(jnp.int32, (rows, 1), 0)
        base = jnp.zeros((rows, 1), jnp.int32)
        for k in range(1, nd):
            base = base + jnp.where(row >= k * cap, tokens, 0)
        col = lax.broadcasted_iota(jnp.int32, (rows, group), 1)
        for q in range(po):
            meta = buf[q, span, width:width + META].astype(jnp.float32)
            hit = col == meta[:, 0:1].astype(jnp.int32) + base
            chi[q] = jnp.where(hit, meta[:, 1:2], 0.0).astype(jnp.bfloat16)
            clo[q] = jnp.where(hit, meta[:, 2:3], 0.0).astype(jnp.bfloat16)
            c_ref[q] = c_ref[q] + jnp.sum(meta[:, 3:4], axis=0, keepdims=True)

        @pl.loop(0, cols // TILE)
        def _(t):
            cs = pl.ds(pl.multiple_of(t * TILE, TILE), TILE)
            acc = jnp.zeros((group, TILE), jnp.float32)
            for q in range(po):
                h = jnp.dot(
                    buf[q, span, 0:width], w[q, :, cs], preferred_element_type=jnp.float32
                ).astype(jnp.bfloat16)
                for part in (chi, clo):
                    acc = acc + lax.dot_general(
                        part[q], h, (((0,), (0,)), ((), ())),
                        preferred_element_type=jnp.float32,
                    )

            @pl.when(mine)
            def _():
                keep[zi, :, cs] = acc

            @pl.when(jnp.logical_not(mine))
            def _():
                sendy[zi, :, cs] = acc.astype(jnp.bfloat16)

        @pl.when(jnp.logical_not(mine))
        def _():
            to_pair(zi).start()

            @pl.when(i >= 3)
            def _():
                zp, _ = source_of(i - 2)
                from_pair(zp)
                sendz[zp] = (keep[zp] + recvy[zp].astype(jnp.float32)).astype(jnp.bfloat16)
                to_line(zp).start()

    load_w.wait()

    def step(i, carry):
        @pl.when(i < ne)
        def _():
            _, ee = source_of(i)

            @pl.when(i != ne - 2)
            def _():
                arrived(d, ee)

            for j in range(nx - 1):
                to_x(i, j, ee).start()
            to_core(i, 0, ee).start()

        @pl.when(jnp.logical_and(i >= 1, i < ne + 1))
        def _():
            _, ee = source_of(i - 1)
            for j in range(1, nx):
                arrived(lax.rem(x + j, nx) * 2 + c, ee)
                to_core(i - 1, j, ee).start()

        @pl.when(i >= 2)
        def _():
            _, ee = source_of(i - 2)
            for j in range(nx):
                arrived(lax.rem(x + j, nx) * 2 + 1 - c, ee)
            work(i - 2)

        return carry

    lax.fori_loop(0, ne + 2, step, 0)

    block = g_ref.shape[1]
    for q in range(po):
        @pl.loop(0, width // TILE)
        def _(t):
            cs = pl.ds(pl.multiple_of(t * TILE, TILE), TILE)
            g_ref[q, :, cs] = lax.dot_general(
                buf[q, :, pl.ds(pl.multiple_of(d * block, block), block)],
                buf[q, :, cs],
                (((0,), (0,)), ((), ())),
                preferred_element_type=jnp.float32,
            )

    from_pair(z)
    for k in range(1, nz):
        zk = lax.rem(z + k, nz)
        remote(sendz.at[zk], recvz.at[zk], zsend.at[zk], zrecv.at[zk], d, e).wait_recv()

    @pl.loop(0, nd)
    def _(k):
        rs = pl.ds(pl.multiple_of(k * tokens, tokens), tokens)
        total = keep[z, rs, :] + recvy[z, rs, :].astype(jnp.float32)
        for j in range(1, nz):
            total = total + recvz[lax.rem(z + j, nz), rs, :].astype(jnp.float32)
        fin[k] = total.astype(jnp.bfloat16)

    def to_token(k):
        dd = lax.rem(d + k, nd)
        return remote(fin.at[dd], osc.at[d], osend.at[k], orecv.at[d], dd, e)

    for k in range(1, nd):
        to_token(k).start()
    o_ref[:, pl.ds(pl.multiple_of(d * cols, cols), cols)] = fin[d]
    for k in range(1, nd):
        dd = lax.rem(d + k, nd)
        remote(fin.at[dd], osc.at[dd], osend.at[k], orecv.at[dd], d, e).wait_recv()
        o_ref[:, pl.ds(pl.multiple_of(dd * cols, cols), cols)] = osc[dd]

    for i in range(ne):
        if i != ne - 2:
            first(i).wait_send()

    def drain(i, carry):
        _, ee = source_of(i)
        for j in range(nx - 1):
            to_x(i, j, ee).wait_send()
        for j in range(nx):
            to_core(i, j, ee).wait_send()
        return carry

    lax.fori_loop(0, ne, drain, 0)
    for k in range(nz):
        to_pair(k).wait_send()
    for k in range(1, nz):
        to_line(lax.rem(z + k, nz)).wait_send()
    for k in range(1, nd):
        to_token(k).wait_send()


def positions(routes, experts):
    flat_routes = routes.reshape(-1)
    onehot = (flat_routes[:, None] == jnp.arange(experts, dtype=jnp.int32)[None, :]).astype(
        jnp.int32
    )
    before = jnp.cumsum(onehot, axis=0) - onehot
    return flat_routes, onehot, jnp.sum(before * onehot, axis=1)


def fused(hidden, routes, gate_scores, down_weight):
    tokens, top_count, width = hidden.shape
    ne, nd = lax.axis_size("expert"), lax.axis_size("dp")
    po, _, cols = down_weight.shape
    experts = ne * po
    pairs = tokens * top_count
    cap = 3 * pairs // (2 * experts)
    flat_routes, _, position = positions(routes, experts)
    slot_index = flat_routes * cap + position
    scores = gate_scores.astype(jnp.float32)
    weight = (scores / jnp.sum(scores, axis=1, keepdims=True)).reshape(pairs)
    hi = weight.astype(jnp.bfloat16)
    lo = (weight - hi.astype(jnp.float32)).astype(jnp.bfloat16)
    token = (jnp.arange(pairs, dtype=jnp.int32) // top_count).astype(jnp.bfloat16)
    meta = jnp.stack([token, hi, lo, jnp.ones_like(hi)], axis=1)
    meta = jnp.pad(meta, ((0, 0), (0, META - 4)))
    pick = (
        jnp.arange(experts * cap, dtype=jnp.int32)[:, None] == slot_index[None, :]
    ).astype(jnp.bfloat16)
    packed = jnp.concatenate([hidden.reshape(pairs, width), meta], axis=1)
    outgoing = jnp.dot(pick, packed, preferred_element_type=jnp.float32).astype(jnp.bfloat16)
    outgoing = outgoing.reshape(experts, cap, width + META)

    nz, nx, group = ne // 2, nd // 2, nd * tokens
    bf, f32 = jnp.bfloat16, jnp.float32
    dma = pltpu.SemaphoreType.DMA
    any_space = pl.BlockSpec(memory_space=pl.ANY)
    vmem = pl.BlockSpec(memory_space=pltpu.VMEM)
    out, gram, count = pl.pallas_call(
        functools.partial(fused_kernel, nd, ne, tokens, cap, width),
        out_shape=(
            jax.ShapeDtypeStruct((tokens, nd * cols), bf),
            jax.ShapeDtypeStruct((po, width // nd, width), f32),
            jax.ShapeDtypeStruct((po, 8, 128), f32),
        ),
        in_specs=[vmem, any_space],
        out_specs=(vmem, vmem, vmem),
        scratch_shapes=[
            pltpu.VMEM((po, ne * nd * cap, width + META), bf),
            pltpu.VMEM((po, width, cols), bf),
            pltpu.VMEM((nz, group, cols), bf),
            pltpu.VMEM((nz, group, cols), bf),
            pltpu.VMEM((nz, group, cols), f32),
            pltpu.VMEM((nz, group, cols), bf),
            pltpu.VMEM((nz, group, cols), bf),
            pltpu.VMEM((nd, tokens, cols), bf),
            pltpu.VMEM((nd, tokens, cols), bf),
            pltpu.VMEM((po, nd * cap, group), bf),
            pltpu.VMEM((po, nd * cap, group), bf),
            dma, dma,
            dma((ne,)), dma((ne, max(nx - 1, 1))), dma((ne, nx)), dma((ne * nd,)),
            dma((nz,)), dma((nz,)), dma((nz,)), dma((nz,)), dma((nd,)), dma((nd,)),
        ],
        compiler_params=pltpu.CompilerParams(
            collective_id=0, has_side_effects=True, vmem_limit_bytes=VMEM_LIMIT
        ),
    )(outgoing, down_weight)
    return out, gram / count[:, :1, :1]


def plain(hidden, routes, gate_scores, down_weight):
    tokens = hidden.shape[0]
    top_count = hidden.shape[1]
    hidden_width = hidden.shape[2]
    n_owner = lax.axis_size("expert")
    n_group = lax.axis_size("dp")
    per_owner = down_weight.shape[0]
    experts = n_owner * per_owner
    pair_total = tokens * top_count
    capacity = 3 * tokens * top_count // (2 * experts)
    flat_routes = routes.reshape(pair_total)
    onehot = (flat_routes[:, None] == jnp.arange(experts, dtype=jnp.int32)[None, :]).astype(
        jnp.int32
    )
    before = jnp.cumsum(onehot, axis=0) - onehot
    position = jnp.sum(before * onehot, axis=1)
    slot_index = flat_routes * capacity + position
    local_counts = jnp.sum(onehot, axis=0).astype(jnp.float32)
    totals = lax.psum(local_counts, ("dp", "expert"))
    pair_rows = hidden.reshape(pair_total, hidden_width)
    outgoing = (
        jnp.zeros((experts * capacity, hidden_width), jnp.bfloat16).at[slot_index].set(pair_rows)
    )
    outgoing = outgoing.reshape(n_owner, per_owner, capacity, hidden_width)
    arrived = lax.all_to_all(outgoing, "expert", split_axis=0, concat_axis=0, tiled=True)
    everyone = lax.all_gather(arrived, "dp", axis=0, tiled=True)
    own_counts = lax.dynamic_slice_in_dim(
        totals, lax.axis_index("expert") * per_owner, per_owner, 0
    )
    block_width = hidden_width // n_group
    my_columns = lax.dynamic_slice_in_dim(
        everyone, lax.axis_index("dp") * block_width, block_width, 3
    )
    gram_rows = jnp.einsum(
        "sxcf,sxcg->xfg", my_columns, everyone, preferred_element_type=jnp.float32
    )
    results = jnp.einsum(
        "sxcf,xfd->sxcd", everyone, down_weight, preferred_element_type=jnp.float32
    ).astype(jnp.bfloat16)
    returned = lax.all_to_all(
        lax.all_to_all(results, "dp", split_axis=0, concat_axis=3, tiled=True),
        "expert",
        split_axis=0,
        concat_axis=0,
        tiled=True,
    )
    gram = gram_rows / own_counts[:, None, None]
    model_width = returned.shape[3]
    pair_results = returned.reshape(experts * capacity, model_width)[slot_index]
    scores = gate_scores.astype(jnp.float32)
    weight = scores / jnp.sum(scores, axis=1, keepdims=True)
    combined = jnp.sum(
        pair_results.reshape(tokens, top_count, model_width).astype(jnp.float32)
        * weight[:, :, None],
        axis=1,
    )
    return (combined.astype(jnp.bfloat16), gram)


def fits(hidden, down_weight, nd, ne):
    tokens, top_count, width = hidden.shape
    po, _, cols = down_weight.shape
    cap = 3 * tokens * top_count // (2 * ne * po)
    group = nd * tokens
    if cap % 16 or tokens % 16 or nd % 2 or ne % 2 or ne < 4 or tokens > 256:
        return False
    if width % TILE or cols % TILE or (width // nd) % 128:
        return False
    need = (
        2 * po * ne * cap * (nd + 1) * (width + META)
        + 2 * po * width * cols
        + (ne // 2) * group * cols * 12
        + 4 * po * (width // nd) * width
        + 6 * group * cols
        + 4 * po * nd * cap * group
    )
    return need <= VMEM_BUDGET


def local(hidden, routes, gate_scores, down_weight):
    if fits(hidden, down_weight, lax.axis_size("dp"), lax.axis_size("expert")):
        return fused(hidden, routes, gate_scores, down_weight)
    return plain(hidden, routes, gate_scores, down_weight)


def solution(mesh):
    placed = (
        P(("dp", "expert"), None, None),
        P(("dp", "expert"), None),
        P(("dp", "expert"), None),
        P("expert", None, "dp"),
    )
    return jax.shard_map(
        local,
        mesh=mesh,
        in_specs=placed,
        out_specs=(P(("dp", "expert"), None), P("expert", "dp", None)),
        check_vma=False,
    )
```

```python
import functools

import jax
import jax.numpy as jnp
from jax import lax
from jax.experimental import pallas as pl
from jax.experimental.pallas import tpu as pltpu
from jax.sharding import PartitionSpec as P

MESH = pl.DeviceIdType.MESH
META = 128
TILE = 256
VMEM_BUDGET = 58 * 2**20
VMEM_LIMIT = 63 * 2**20


def fused_kernel(
    nd, ne, tokens, cap, width,
    og, w_hbm, o_ref, g_ref, c_ref,
    buf, w, sendy, recvy, keep, sendz, recvz, fin, osc, chi, clo,
    wsem, lsem, asend, xsend, csend, recv, ysend, yrecv, zsend, zrecv, osend, orecv,
):
    po = w.shape[0]
    nz = ne // 2
    nx = nd // 2
    rows = nd * cap
    group = nd * tokens
    cols = w.shape[2]
    d = lax.axis_index("dp")
    e = lax.axis_index("expert")
    x, c = lax.div(d, 2), lax.rem(d, 2)
    z, y = lax.div(e, 2), lax.rem(e, 2)
    other = d + 1 - 2 * c
    pair = e + 1 - 2 * y

    load_w = pltpu.make_async_copy(w_hbm, w, wsem)
    load_w.start()

    def slot_of(dd, ee):
        return buf.at[:, pl.ds(pl.multiple_of((ee * nd + dd) * cap, cap), cap), :]

    own = pltpu.make_async_copy(
        og.at[pl.ds(e * po, po)], slot_of(d, e), lsem
    )
    own.start()

    barrier = pltpu.get_barrier_semaphore()
    for k in range(1, ne):
        pl.semaphore_signal(
            barrier, inc=1, device_id=(d, lax.rem(e + k, ne)), device_id_type=MESH
        )
    for k in range(1, nd):
        pl.semaphore_signal(
            barrier, inc=1, device_id=(lax.rem(d + k, nd), e), device_id_type=MESH
        )
    pl.semaphore_wait(barrier, ne - 1 + nd - 1)

    def remote(src, dst, ss, rs, dd, ee):
        return pltpu.make_async_remote_copy(
            src_ref=src, dst_ref=dst, send_sem=ss, recv_sem=rs,
            device_id=(dd, ee), device_id_type=MESH,
        )

    near = z + 1 - 2 * lax.rem(z, 2)
    far = lax.rem(z + 2, nz)

    def source_of(i):
        j = lax.div(i, 2)
        flip = lax.rem(j, 2) * (1 - 2 * lax.rem(z, 2))
        zi = lax.rem(z + flip + 2 * lax.rem(lax.div(j + 1, 2), 2), nz)
        return zi, zi * 2 + lax.rem(y + lax.rem(i, 2), 2)

    def first(i):
        _, target = source_of(jnp.int32(i))
        return remote(
            og.at[pl.ds(target * po, po)], slot_of(d, e), asend.at[i],
            recv.at[e * nd + d], d, target,
        )

    for i in range(1, ne):
        first(i).start()
    own.wait()
    c_ref[...] = jnp.zeros_like(c_ref)
    g_ref[...] = jnp.zeros_like(g_ref)

    def arrived(dd, ee):
        here = slot_of(dd, ee)
        remote(here, here, asend.at[0], recv.at[ee * nd + dd], d, e).wait_recv()

    def to_x(i, j, ee):
        here = slot_of(d, ee)
        return remote(
            here, here, xsend.at[i, j], recv.at[ee * nd + d],
            lax.rem(x + j + 1, nx) * 2 + c, e,
        )

    def to_core(i, j, ee):
        dd = lax.rem(x + j, nx) * 2 + c
        here = slot_of(dd, ee)
        return remote(here, here, csend.at[i, j], recv.at[ee * nd + dd], other, e)

    def chunk(k):
        return pl.ds(pl.multiple_of(k * tokens, tokens), tokens)

    def to_pair(zi, k):
        return remote(
            sendy.at[zi, chunk(k)], recvy.at[zi, chunk(k)],
            ysend.at[zi, k], yrecv.at[zi, k], d, pair,
        )

    def from_pair(zi, k):
        remote(
            sendy.at[zi, chunk(k)], recvy.at[zi, chunk(k)],
            ysend.at[zi, k], yrecv.at[zi, k], d, e,
        ).wait_recv()

    def to_line(m, k, zt):
        return remote(
            sendz.at[m, chunk(k)], recvz.at[m, chunk(k)],
            zsend.at[m, k], zrecv.at[m, k], d, zt * 2 + y,
        )

    def from_line(m, k):
        remote(
            sendz.at[m, chunk(k)], recvz.at[m, chunk(k)],
            zsend.at[m, k], zrecv.at[m, k], d, e,
        ).wait_recv()

    def both(zi, k):
        return keep[zi, chunk(k), :] + recvy[zi, chunk(k), :].astype(jnp.float32)

    def chunks(body):
        def at(k, carry):
            body(lax.rem(d + 1 + k, nd))
            return carry

        lax.fori_loop(0, nd, at, 0)

    def work(i):
        zi, ee = source_of(i)
        mine = lax.rem(i, 2) == 0
        span = pl.ds(pl.multiple_of(ee * rows, rows), rows)
        row = lax.broadcasted_iota(jnp.int32, (rows, 1), 0)
        base = jnp.zeros((rows, 1), jnp.int32)
        for k in range(1, nd):
            base = base + jnp.where(row >= k * cap, tokens, 0)
        col = lax.broadcasted_iota(jnp.int32, (rows, group), 1)
        for q in range(po):
            meta = buf[q, span, width:width + META].astype(jnp.float32)
            hit = col == meta[:, 0:1].astype(jnp.int32) + base
            chi[q] = jnp.where(hit, meta[:, 1:2], 0.0).astype(jnp.bfloat16)
            clo[q] = jnp.where(hit, meta[:, 2:3], 0.0).astype(jnp.bfloat16)
            c_ref[q] = c_ref[q] + jnp.sum(meta[:, 3:4], axis=0, keepdims=True)

        @pl.loop(0, cols // TILE)
        def _(t):
            cs = pl.ds(pl.multiple_of(t * TILE, TILE), TILE)
            acc = jnp.zeros((group, TILE), jnp.float32)
            for q in range(po):
                h = jnp.dot(
                    buf[q, span, 0:width], w[q, :, cs], preferred_element_type=jnp.float32
                ).astype(jnp.bfloat16)
                for part in (chi, clo):
                    acc = acc + lax.dot_general(
                        part[q], h, (((0,), (0,)), ((), ())),
                        preferred_element_type=jnp.float32,
                    )

            @pl.when(mine)
            def _():
                keep[zi, :, cs] = acc

            @pl.when(jnp.logical_not(mine))
            def _():
                sendy[zi, :, cs] = acc.astype(jnp.bfloat16)

        @pl.when(jnp.logical_not(mine))
        def _():
            chunks(lambda k: to_pair(zi, k).start())

        @pl.when(i == 4)
        def _():
            def go(k):
                zp = lax.rem(near + 2, nz)
                from_pair(zp, k)
                sendz[0, chunk(k), :] = both(zp, k).astype(jnp.bfloat16)
                to_line(0, k, near).start()

            chunks(go)

        @pl.when(i == 6)
        def _():
            def go(k):
                from_pair(far, k)
                from_line(0, k)
                sendz[1, chunk(k), :] = (
                    both(far, k) + recvz[0, chunk(k), :].astype(jnp.float32)
                ).astype(jnp.bfloat16)
                to_line(1, k, far).start()

            chunks(go)

        block = g_ref.shape[1]
        for q in range(po):
            @pl.loop(0, width // TILE)
            def _(t):
                cs = pl.ds(pl.multiple_of(t * TILE, TILE), TILE)
                g_ref[q, :, cs] += lax.dot_general(
                    buf[q, span, pl.ds(pl.multiple_of(d * block, block), block)],
                    buf[q, span, cs],
                    (((0,), (0,)), ((), ())),
                    preferred_element_type=jnp.float32,
                )

    load_w.wait()

    def step(i, carry):
        @pl.when(i < ne)
        def _():
            _, ee = source_of(i)

            @pl.when(i != 0)
            def _():
                arrived(d, ee)

            for j in range(nx - 1):
                to_x(i, j, ee).start()
            to_core(i, 0, ee).start()

        @pl.when(jnp.logical_and(i >= 1, i < ne + 1))
        def _():
            _, ee = source_of(i - 1)
            for j in range(1, nx):
                arrived(lax.rem(x + j, nx) * 2 + c, ee)
                to_core(i - 1, j, ee).start()

        @pl.when(i >= 2)
        def _():
            _, ee = source_of(i - 2)
            for j in range(nx):
                arrived(lax.rem(x + j, nx) * 2 + 1 - c, ee)
            work(i - 2)

        return carry

    lax.fori_loop(0, ne + 2, step, 0)

    def pass_on(k):
        from_pair(near, k)
        sendz[2, chunk(k), :] = both(near, k).astype(jnp.bfloat16)
        to_line(2, k, near).start()

    chunks(pass_on)

    def to_token(dd):
        return remote(fin.at[dd], osc.at[d], osend.at[dd], orecv.at[d], dd, e)

    def settle(dd):
        from_pair(z, dd)
        from_line(1, dd)
        from_line(2, dd)
        total = both(z, dd) + recvz[1, chunk(dd), :].astype(jnp.float32)
        total = total + recvz[2, chunk(dd), :].astype(jnp.float32)
        fin[dd] = total.astype(jnp.bfloat16)

        @pl.when(dd != d)
        def _():
            to_token(dd).start()

    chunks(settle)
    o_ref[:, pl.ds(pl.multiple_of(d * cols, cols), cols)] = fin[d]
    for k in range(1, nd):
        dd = lax.rem(d + k, nd)
        remote(fin.at[dd], osc.at[dd], osend.at[dd], orecv.at[dd], d, e).wait_recv()
        o_ref[:, pl.ds(pl.multiple_of(dd * cols, cols), cols)] = osc[dd]

    for i in range(1, ne):
        first(i).wait_send()

    def drain(i, carry):
        _, ee = source_of(i)
        for j in range(nx - 1):
            to_x(i, j, ee).wait_send()
        for j in range(nx):
            to_core(i, j, ee).wait_send()
        return carry

    lax.fori_loop(0, ne, drain, 0)
    def sent(k):
        for zi in range(nz):
            to_pair(zi, k).wait_send()
        to_line(0, k, near).wait_send()
        to_line(1, k, far).wait_send()
        to_line(2, k, near).wait_send()

    chunks(sent)
    for k in range(1, nd):
        to_token(lax.rem(d + k, nd)).wait_send()


def positions(routes, experts):
    flat_routes = routes.reshape(-1)
    onehot = (flat_routes[:, None] == jnp.arange(experts, dtype=jnp.int32)[None, :]).astype(
        jnp.int32
    )
    before = jnp.cumsum(onehot, axis=0) - onehot
    return flat_routes, onehot, jnp.sum(before * onehot, axis=1)


def fused(hidden, routes, gate_scores, down_weight):
    tokens, top_count, width = hidden.shape
    ne, nd = lax.axis_size("expert"), lax.axis_size("dp")
    po, _, cols = down_weight.shape
    experts = ne * po
    pairs = tokens * top_count
    cap = 3 * pairs // (2 * experts)
    flat_routes, _, position = positions(routes, experts)
    slot_index = flat_routes * cap + position
    scores = gate_scores.astype(jnp.float32)
    weight = (scores / jnp.sum(scores, axis=1, keepdims=True)).reshape(pairs)
    hi = weight.astype(jnp.bfloat16)
    lo = (weight - hi.astype(jnp.float32)).astype(jnp.bfloat16)
    token = (jnp.arange(pairs, dtype=jnp.int32) // top_count).astype(jnp.bfloat16)
    meta = jnp.stack([token, hi, lo, jnp.ones_like(hi)], axis=1)
    meta = jnp.pad(meta, ((0, 0), (0, META - 4)))
    pick = (
        jnp.arange(experts * cap, dtype=jnp.int32)[:, None] == slot_index[None, :]
    ).astype(jnp.bfloat16)
    packed = jnp.concatenate([hidden.reshape(pairs, width), meta], axis=1)
    outgoing = jnp.dot(pick, packed, preferred_element_type=jnp.float32).astype(jnp.bfloat16)
    outgoing = outgoing.reshape(experts, cap, width + META)

    nz, nx, group = ne // 2, nd // 2, nd * tokens
    bf, f32 = jnp.bfloat16, jnp.float32
    dma = pltpu.SemaphoreType.DMA
    any_space = pl.BlockSpec(memory_space=pl.ANY)
    vmem = pl.BlockSpec(memory_space=pltpu.VMEM)
    out, gram, count = pl.pallas_call(
        functools.partial(fused_kernel, nd, ne, tokens, cap, width),
        out_shape=(
            jax.ShapeDtypeStruct((tokens, nd * cols), bf),
            jax.ShapeDtypeStruct((po, width // nd, width), f32),
            jax.ShapeDtypeStruct((po, 8, 128), f32),
        ),
        in_specs=[vmem, any_space],
        out_specs=(vmem, vmem, vmem),
        scratch_shapes=[
            pltpu.VMEM((po, ne * nd * cap, width + META), bf),
            pltpu.VMEM((po, width, cols), bf),
            pltpu.VMEM((nz, group, cols), bf),
            pltpu.VMEM((nz, group, cols), bf),
            pltpu.VMEM((nz, group, cols), f32),
            pltpu.VMEM((3, group, cols), bf),
            pltpu.VMEM((3, group, cols), bf),
            pltpu.VMEM((nd, tokens, cols), bf),
            pltpu.VMEM((nd, tokens, cols), bf),
            pltpu.VMEM((po, nd * cap, group), bf),
            pltpu.VMEM((po, nd * cap, group), bf),
            dma, dma,
            dma((ne,)), dma((ne, max(nx - 1, 1))), dma((ne, nx)), dma((ne * nd,)),
            dma((nz, nd)), dma((nz, nd)), dma((3, nd)), dma((3, nd)), dma((nd,)), dma((nd,)),
        ],
        compiler_params=pltpu.CompilerParams(
            collective_id=0, has_side_effects=True, vmem_limit_bytes=VMEM_LIMIT
        ),
    )(outgoing, down_weight)
    return out, gram / count[:, :1, :1]


def plain(hidden, routes, gate_scores, down_weight):
    tokens = hidden.shape[0]
    top_count = hidden.shape[1]
    hidden_width = hidden.shape[2]
    n_owner = lax.axis_size("expert")
    n_group = lax.axis_size("dp")
    per_owner = down_weight.shape[0]
    experts = n_owner * per_owner
    pair_total = tokens * top_count
    capacity = 3 * tokens * top_count // (2 * experts)
    flat_routes = routes.reshape(pair_total)
    onehot = (flat_routes[:, None] == jnp.arange(experts, dtype=jnp.int32)[None, :]).astype(
        jnp.int32
    )
    before = jnp.cumsum(onehot, axis=0) - onehot
    position = jnp.sum(before * onehot, axis=1)
    slot_index = flat_routes * capacity + position
    local_counts = jnp.sum(onehot, axis=0).astype(jnp.float32)
    totals = lax.psum(local_counts, ("dp", "expert"))
    pair_rows = hidden.reshape(pair_total, hidden_width)
    outgoing = (
        jnp.zeros((experts * capacity, hidden_width), jnp.bfloat16).at[slot_index].set(pair_rows)
    )
    outgoing = outgoing.reshape(n_owner, per_owner, capacity, hidden_width)
    arrived = lax.all_to_all(outgoing, "expert", split_axis=0, concat_axis=0, tiled=True)
    everyone = lax.all_gather(arrived, "dp", axis=0, tiled=True)
    own_counts = lax.dynamic_slice_in_dim(
        totals, lax.axis_index("expert") * per_owner, per_owner, 0
    )
    block_width = hidden_width // n_group
    my_columns = lax.dynamic_slice_in_dim(
        everyone, lax.axis_index("dp") * block_width, block_width, 3
    )
    gram_rows = jnp.einsum(
        "sxcf,sxcg->xfg", my_columns, everyone, preferred_element_type=jnp.float32
    )
    results = jnp.einsum(
        "sxcf,xfd->sxcd", everyone, down_weight, preferred_element_type=jnp.float32
    ).astype(jnp.bfloat16)
    returned = lax.all_to_all(
        lax.all_to_all(results, "dp", split_axis=0, concat_axis=3, tiled=True),
        "expert",
        split_axis=0,
        concat_axis=0,
        tiled=True,
    )
    gram = gram_rows / own_counts[:, None, None]
    model_width = returned.shape[3]
    pair_results = returned.reshape(experts * capacity, model_width)[slot_index]
    scores = gate_scores.astype(jnp.float32)
    weight = scores / jnp.sum(scores, axis=1, keepdims=True)
    combined = jnp.sum(
        pair_results.reshape(tokens, top_count, model_width).astype(jnp.float32)
        * weight[:, :, None],
        axis=1,
    )
    return (combined.astype(jnp.bfloat16), gram)


def fits(hidden, down_weight, nd, ne):
    tokens, top_count, width = hidden.shape
    po, _, cols = down_weight.shape
    cap = 3 * tokens * top_count // (2 * ne * po)
    group = nd * tokens
    if cap % 16 or tokens % 16 or nd % 2 or ne != 8 or tokens > 256:
        return False
    if width % TILE or cols % TILE or (width // nd) % 128:
        return False
    need = (
        2 * po * ne * cap * (nd + 1) * (width + META)
        + 2 * po * width * cols
        + (ne // 2) * group * cols * 12
        + 4 * po * (width // nd) * width
        + 6 * group * cols
        + 4 * po * nd * cap * group
    )
    return need <= VMEM_BUDGET


def local(hidden, routes, gate_scores, down_weight):
    if fits(hidden, down_weight, lax.axis_size("dp"), lax.axis_size("expert")):
        return fused(hidden, routes, gate_scores, down_weight)
    return plain(hidden, routes, gate_scores, down_weight)


def solution(mesh):
    placed = (
        P(("dp", "expert"), None, None),
        P(("dp", "expert"), None),
        P(("dp", "expert"), None),
        P("expert", None, "dp"),
    )
    return jax.shard_map(
        local,
        mesh=mesh,
        in_specs=placed,
        out_specs=(P(("dp", "expert"), None), P("expert", "dp", None)),
        check_vma=False,
    )
```
